128 devices in a mesh: req: 8 (over z, core), exp: 16 (over y, x).
Axes of the slice: x: 4, y: 4, z: 4, core: 2. Of those that a mesh axis runs over, the one named last changes fastest.
Arguments:
- hidden: bfloat16 [16384, 2048], P(('req', 'exp')), may hold values from -6 to 6
- attn_gain: float32 [2048], replicated, may hold values from 0.5 to 1.5
- w_query: bfloat16 [2048, 2048], P(None, 'exp'), may hold values from -0.125 to 0.125
- w_keyval: bfloat16 [2, 2048, 2048], P(None, None, 'exp'), may hold values from -0.3125 to 0.3125
- k_pool: bfloat16 [1280, 128, 2048], P('req', None, 'exp'), may hold values from -86 to 86
- v_pool: bfloat16 [1280, 128, 2048], P('req', None, 'exp'), may hold values from -16 to 16
- dec_len: int32 [32], P('req'), may hold values from 1 to 4096, as said below
- dec_pages: int32 [32, 32], P('req'), may hold values from 0 to 159, as said below
- pre_pos: int32 [8], P('req'), may hold values from 0 to 4096, as said below
- pre_pages: int32 [8, 32], P('req'), may hold values from 0 to 159
- w_out: bfloat16 [2048, 2048], P('exp'), may hold values from -0.125 to 0.125
- moe_gain: float32 [2048], replicated, may hold values from 0.1 to 1.9
- expert_ids: int32 [16384, 8], P(('req', 'exp')), may hold values from 0 to 63, all different within a row; in each aligned block of 128 rows (0 to 127, 128 to 255, ...) at most 20 rows name the same one
- router_logits: float32 [16384, 8], P(('req', 'exp')), may hold values from -0.4 to 283
- w_in: bfloat16 [128, 2048, 1024], P(('req', 'exp')), may hold values from -0.125 to 0.125
- w_down: bfloat16 [128, 512, 2048], P(('req', 'exp')), may hold values from -0.25 to 0.25
Outputs:
- mixed: bfloat16 [16384, 2048], P(('req', 'exp'))
- new_kv: bfloat16 [2, 16384, 2048], P(None, 'req', 'exp')
The draws below stay inside these ranges and needn't reach their ends.
Inputs may be any that keep to these rules, and one draw needn't show every extreme that they name: Within each group, the rows of dec_pages of its 4 requests and its row of pre_pages name every one of the group's 160 pages exactly once. `dec_len`: some request has exactly 4096 cached positions. `pre_pos`: some group's prefix has exactly 4096 positions. `expert_ids`: each row names 8 different experts; among the rows of one device no expert is named by more than 20 rows.
All inputs are finite; a program needn't handle non-finite values.
Results may differ from the reference program's by a relative error of at most 0.02.
Values may be sent and summed in bfloat16 or wider, within the bound.
A program may use at most 128 MiB of HBM per device.

```python
import math
import jax
import jax.numpy as jnp
import numpy as np
from jax import lax

D = 2048
HD = 128
FF = 1024
TOPK = 8
SPLIT = 2
PAGE = 128
DEC_GRP = 4
DEC_PAGES = 32
TOK_DEV = 128
HEADS = 16
EXPERTS = 64
CAP = 20
TOKENS = 16384
PAGES = 160
DEC_MAX = 4096
PRE_MAX = 4096
N_REQ = 8
N_EXP = 16


def pool_tables(key):

    def one_group(group):
        return jax.random.permutation(jax.random.fold_in(key, group), PAGES).astype(jnp.int32)
    return jax.vmap(one_group)(jnp.arange(N_REQ, dtype=jnp.int32))


def draw_dec_pages(key, part):
    tables = pool_tables(jax.random.fold_in(key, 11))
    return tables[:, :DEC_GRP * DEC_PAGES].reshape(N_REQ * DEC_GRP, DEC_PAGES)


def draw_pre_pages(key, part):
    tables = pool_tables(jax.random.fold_in(key, 11))
    return tables[:, DEC_GRP * DEC_PAGES:]


def draw_dec_len(key, part):
    first, second = jax.random.split(jax.random.fold_in(key, 21))
    lengths = jax.random.randint(first, (N_REQ * DEC_GRP,), 1, DEC_MAX + 1)
    where = jax.random.randint(second, (), 0, N_REQ * DEC_GRP)
    return lengths.at[where].set(DEC_MAX).astype(jnp.int32)


def draw_pre_pos(key, part):
    first, second = jax.random.split(jax.random.fold_in(key, 23))
    starts = jax.random.randint(first, (N_REQ,), 0, PRE_MAX + 1)
    where = jax.random.randint(second, (), 0, N_REQ)
    return starts.at[where].set(PRE_MAX).astype(jnp.int32)


def draw_k_pool(key, part):
    first = jax.random.fold_in(jax.random.fold_in(key, 31), 0)
    shape = (N_REQ * PAGES, PAGE, HEADS * HD)
    return (jnp.clip(jax.random.normal(first, shape, jnp.float32), -6.0, 6.0) * 2.5).astype(jnp.bfloat16)


def draw_router_logits(key, part):
    first = jax.random.fold_in(jax.random.fold_in(key, 41), 0)
    shape = (TOKENS, TOPK)
    return jax.random.uniform(first, shape, jnp.float32, -0.4, 0.4)


def block_levels(stream_key, dims, cuts, least, top_value):
    level = 1.0
    for axis_at, parts in cuts:
        draws = jax.random.uniform(jax.random.fold_in(jax.random.fold_in(stream_key, 6), axis_at), (parts,), jnp.float32, least / len(cuts), top_value / len(cuts))
        level = level * jnp.repeat(jnp.exp(draws), dims[axis_at] // parts).reshape((-1,) + (1,) * (len(dims) - 1 - axis_at))
    return level


def assign_block(key, own, number, rows, count, top, most, skew):
    order = jax.random.permutation(key, count)
    heavy_load, ordinary = shares(count, rows * top, most, skew, True), shares(count, rows * top, most, skew, False)
    places = jnp.arange(count)

    def named(tallies, rotation):
        used = int((tallies > 0).sum())
        fixed = max(1, used // 4)
        shifted = fixed + (places - fixed + rotation * (used - fixed)) % max(1, count - fixed)
        return jnp.zeros((count,), jnp.int32).at[order[jnp.where(places < fixed, places, shifted)]].set(jnp.asarray(tallies, jnp.int32))

    tallies = jnp.where(number % 4 == 0, named(heavy_load, number // 4), named(ordinary, number - number // 4 - 1))
    mixed = jax.random.permutation(jax.random.fold_in(own, 3), count)
    donor, taker = mixed[0:count // 2 * 2:2], mixed[1:count // 2 * 2:2]
    room = jnp.minimum(tallies[donor] - 1, most - tallies[taker]) // 2
    room = jnp.where((donor == order[0]) | (taker == order[0]) | (tallies[taker] == 0), 0, jnp.maximum(room, 0))
    shifted = jax.random.randint(jax.random.fold_in(own, 4), (count // 2,), 0, 1 << 20) % (room + 1)
    tallies = tallies.at[donor].add(-shifted).at[taker].add(shifted)
    members = jnp.searchsorted(jnp.cumsum(tallies), jnp.arange(rows * top), side="right").astype(jnp.int32)
    listing = members.reshape(top, rows).T
    listing = listing[jax.random.permutation(jax.random.fold_in(own, 1), rows)]
    rotation = jax.random.randint(jax.random.fold_in(own, 2), (rows, 1), 0, top)
    return jnp.take_along_axis(listing, (jnp.arange(top)[None, :] + rotation) % top, axis=1)


def shares(count, total, reach, skew, full):
    portions = [(1 << 20) // math.isqrt(grade ** skew) + 1 for grade in range(1, count + 1)]
    largest = reach if full else min(reach, max(-(-total // count), total * portions[0] // sum(portions)))
    least = 1 if total - largest >= count - 1 else 0
    holding, spare = [largest] + [least] * (count - 1), total - largest - least * (count - 1)
    while spare > 0:
        free = [i for i in range(1, count) if holding[i] < largest] or [i for i in range(1, count) if holding[i] < reach]
        pool, remaining = sum([portions[i] for i in free]), spare
        for i in free:
            extra = min(reach - holding[i], max(1, remaining * portions[i] // pool), spare)
            holding[i] = holding[i] + extra
            spare = spare - extra
    return np.array(holding)


def noise(key, dims, spread, reach, pieces=(), kind=jnp.bfloat16):
    loudness = block_levels(key, dims, pieces, -0.22, 0.18) if pieces else 1.0
    values = jax.random.normal(key, dims, jnp.float32) * spread * loudness
    return jnp.minimum(jnp.maximum(values, -reach), reach).astype(kind)


def setup_inputs(seed: int = 0) -> dict:
    key_of = jax.random.split(jax.random.key(seed), 17)
    hidden = noise(key_of[0], (TOKENS, D), 1.0, 6.0, ((0, 128),))
    attn_gain = jnp.clip(1.0 + 0.1 * jax.random.normal(key_of[1], (D,), jnp.float32), 0.5, 1.5)
    w_query = noise(key_of[2], (D, HEADS * HD), D ** -0.5, 0.125, ((1, 16),))
    w_keyval = noise(key_of[3], (2, D, HEADS * HD), (2.5 * D ** -0.5), 0.3125, ((2, 16),))
    k_pool = draw_k_pool(jax.random.fold_in(key_of[16], 71), 0)
    v_pool = noise(key_of[5], (N_REQ * PAGES, PAGE, HEADS * HD), 2.5, 16.0, ((0, 8), (2, 16)))
    dec_len = draw_dec_len(jax.random.fold_in(key_of[16], 71), 0)
    dec_pages = draw_dec_pages(jax.random.fold_in(key_of[16], 71), 0)
    pre_pos = draw_pre_pos(jax.random.fold_in(key_of[16], 71), 0)
    pre_pages = draw_pre_pages(jax.random.fold_in(key_of[16], 71), 0)
    w_out = noise(key_of[10], (HEADS * HD, D), (HEADS * HD) ** -0.5, 0.125, ((0, 16),))
    moe_gain = jnp.clip(1.0 + 0.18 * jax.random.normal(key_of[11], (D,), jnp.float32), 0.1, 1.9)
    expert_ids_keys = jax.random.split(jax.random.fold_in(key_of[12], 1), TOKENS // TOK_DEV)
    expert_ids_turns = jax.random.permutation(jax.random.fold_in(key_of[12], 3), TOKENS // TOK_DEV)
    expert_ids = jax.vmap(lambda own, number: assign_block(jax.random.fold_in(key_of[12], 2), own, number, TOK_DEV, EXPERTS, TOPK, CAP, 2))(expert_ids_keys, expert_ids_turns).reshape((TOKENS, TOPK))
    router_logits = draw_router_logits(jax.random.fold_in(key_of[16], 71), 0)
    w_in = noise(key_of[14], (EXPERTS * SPLIT, D, 2 * (FF // SPLIT)), D ** -0.5, 0.125, ((0, 128),))
    w_down = noise(key_of[15], (EXPERTS * SPLIT, FF // SPLIT, D), (FF // SPLIT) ** -0.5, 0.25, ((0, 128),))
    return {"hidden": hidden, "attn_gain": attn_gain, "w_query": w_query, "w_keyval": w_keyval, "k_pool": k_pool, "v_pool": v_pool, "dec_len": dec_len, "dec_pages": dec_pages, "pre_pos": pre_pos, "pre_pages": pre_pages, "w_out": w_out, "moe_gain": moe_gain, "expert_ids": expert_ids, "router_logits": router_logits, "w_in": w_in, "w_down": w_down}


EPSILON = 1e-05
THETA = 10000.0

def rms_scale(inputs, gain):
    values = inputs.astype(jnp.float32)
    mean_square = lax.optimization_barrier(jnp.mean(values * values, axis=-1, keepdims=True))
    return (values * lax.rsqrt(mean_square + EPSILON) * gain).astype(jnp.bfloat16)

def rotate(values, positions):
    head_size = values.shape[-1]
    half = head_size // 2
    steps = jnp.arange(half, dtype=jnp.float32)
    frequency = jnp.exp(steps * (-2.0 * math.log(THETA) / head_size))
    angles = positions.astype(jnp.float32)[:, None, None] * frequency[None, None, :]
    cosine = jnp.cos(angles)
    sine = jnp.sin(angles)
    first = values[..., :half]
    second = values[..., half:]
    return jnp.concatenate([first * cosine - second * sine, second * cosine + first * sine], axis=-1)

def attend(query, keys, values, allowed):
    scores = jnp.dot(query, keys.T, preferred_element_type=jnp.float32) * (1.0 / math.sqrt(query.shape[-1]))
    scores = jnp.where(allowed, scores, -jnp.inf)
    highest = lax.optimization_barrier(jnp.max(scores, axis=1, keepdims=True))
    weights = jnp.exp(scores - highest)
    total = lax.optimization_barrier(jnp.sum(weights, axis=1, keepdims=True))
    summed = jnp.dot(weights.astype(jnp.bfloat16), values, preferred_element_type=jnp.float32)
    return (summed / total).astype(jnp.bfloat16)

def reference(hidden, attn_gain, w_query, w_keyval, k_pool, v_pool, dec_len, dec_pages, pre_pos, pre_pages, w_out, moe_gain, expert_ids, router_logits, w_in, w_down):
    group_rows = TOK_DEV * N_EXP
    segment = group_rows - DEC_GRP
    normed_attn = rms_scale(hidden, attn_gain)
    row_index = jnp.arange(TOKENS, dtype=jnp.int32)
    group_of = row_index // group_rows
    inside = row_index % group_rows
    dec_index = group_of * DEC_GRP + jnp.minimum(inside, DEC_GRP - 1)
    positions = jnp.where(inside < DEC_GRP, dec_len[dec_index], pre_pos[group_of] + inside - DEC_GRP)
    query_all = jnp.dot(normed_attn, w_query, preferred_element_type=jnp.float32).reshape(TOKENS, HEADS, HD)
    keys_all = jnp.dot(normed_attn, w_keyval[0], preferred_element_type=jnp.float32).reshape(TOKENS, HEADS, HD)
    values_all = jnp.dot(normed_attn, w_keyval[1], preferred_element_type=jnp.float32).reshape(TOKENS, HEADS, HD)
    query = rotate(query_all, positions).astype(jnp.bfloat16)
    keys_new = rotate(keys_all, positions).astype(jnp.bfloat16)
    values_new = values_all.astype(jnp.bfloat16)
    new_kv = jnp.stack([keys_new.reshape(TOKENS, HEADS * HD), values_new.reshape(TOKENS, HEADS * HD)])

    def group_attention(group):
        start = group * group_rows
        query_group = lax.dynamic_slice_in_dim(query, start, group_rows, 0)
        keys_group = lax.dynamic_slice_in_dim(keys_new, start, group_rows, 0)
        values_group = lax.dynamic_slice_in_dim(values_new, start, group_rows, 0)
        pool_keys = lax.dynamic_slice_in_dim(k_pool, group * PAGES, PAGES, 0)
        pool_values = lax.dynamic_slice_in_dim(v_pool, group * PAGES, PAGES, 0)
        prefix_table = lax.dynamic_index_in_dim(pre_pages, group, 0, keepdims=False)
        length = lax.dynamic_index_in_dim(pre_pos, group, 0, keepdims=False)
        prefix_keys = pool_keys[prefix_table].reshape(PRE_MAX, HEADS, HD)
        prefix_values = pool_values[prefix_table].reshape(PRE_MAX, HEADS, HD)
        key_slots = jnp.arange(PRE_MAX, dtype=jnp.int32)
        own_slots = jnp.arange(segment, dtype=jnp.int32)
        allowed = jnp.concatenate([jnp.broadcast_to(key_slots[None, :] < length, (segment, PRE_MAX)), own_slots[None, :] <= own_slots[:, None]], axis=1)
        seg_query = query_group[DEC_GRP:]
        seg_keys = jnp.concatenate([prefix_keys, keys_group[DEC_GRP:]], axis=0)
        seg_values = jnp.concatenate([prefix_values, values_group[DEC_GRP:]], axis=0)

        def one_head(items):
            head_query, head_keys, head_values = items
            return attend(head_query, head_keys, head_values, allowed)
        seg_out = lax.map(one_head, (jnp.swapaxes(seg_query, 0, 1), jnp.swapaxes(seg_keys, 0, 1), jnp.swapaxes(seg_values, 0, 1)))
        seg_out = jnp.swapaxes(seg_out, 0, 1).reshape(segment, HEADS * HD)
        dec_tables = lax.dynamic_slice_in_dim(dec_pages, group * DEC_GRP, DEC_GRP, 0)
        dec_limits = lax.dynamic_slice_in_dim(dec_len, group * DEC_GRP, DEC_GRP, 0)
        cache_keys = pool_keys[dec_tables].reshape(DEC_GRP, DEC_MAX, HEADS, HD)
        cache_values = pool_values[dec_tables].reshape(DEC_GRP, DEC_MAX, HEADS, HD)

        def one_request(table_keys, table_values, own_query, own_key, own_value, limit):
            every_key = jnp.concatenate([table_keys, own_key[None]], axis=0)
            every_value = jnp.concatenate([table_values, own_value[None]], axis=0)
            visible = jnp.concatenate([jnp.arange(DEC_MAX, dtype=jnp.int32) < limit, jnp.array([True])])[None, :]
            per_head = jax.vmap(attend, in_axes=(0, 1, 1, None))(own_query[:, None, :], every_key, every_value, visible)
            return per_head.reshape(HEADS * HD)
        decode_out = jax.vmap(one_request)(cache_keys, cache_values, query_group[:DEC_GRP], keys_group[:DEC_GRP], values_group[:DEC_GRP], dec_limits)
        return jnp.concatenate([decode_out, seg_out], axis=0)
    attended = lax.map(group_attention, jnp.arange(N_REQ, dtype=jnp.int32)).reshape(TOKENS, HEADS * HD)
    projected = jnp.zeros((TOKENS, D), jnp.float32)
    for head in range(HEADS):
        term = jnp.dot(attended[:, head * HD:(head + 1) * HD], w_out[head * HD:(head + 1) * HD], preferred_element_type=jnp.float32)
        projected = projected + lax.optimization_barrier(term.astype(jnp.bfloat16)).astype(jnp.float32)
    residual = (hidden.astype(jnp.float32) + projected).astype(jnp.bfloat16)
    normed_moe = rms_scale(residual, moe_gain)
    gates = jax.nn.softmax(router_logits.astype(jnp.float32), axis=-1)
    flat_ids = expert_ids.reshape(-1)
    flat_gates = gates.reshape(-1)
    most = N_REQ * N_EXP * CAP
    piece_units = FF // SPLIT

    def one_piece(total, piece):
        expert = piece // SPLIT
        chosen = flat_ids == expert
        picked = jnp.nonzero(chosen, size=most, fill_value=0)[0].astype(jnp.int32)
        live = jnp.arange(most, dtype=jnp.int32) < jnp.sum(chosen.astype(jnp.int32))
        owners = picked // TOPK
        inputs = normed_moe[owners]
        inner = jnp.dot(inputs, w_in[piece], preferred_element_type=jnp.float32)
        activated = (jax.nn.silu(inner[:, :piece_units]) * inner[:, piece_units:]).astype(jnp.bfloat16)
        partial_value = jnp.dot(activated, w_down[piece], preferred_element_type=jnp.float32).astype(jnp.bfloat16)
        factor = jnp.where(live, flat_gates[picked], 0.0)
        total = total.at[owners].add(factor[:, None] * partial_value.astype(jnp.float32))
        return (total, None)
    moe_out = lax.scan(one_piece, jnp.zeros((TOKENS, D), jnp.float32), jnp.arange(EXPERTS * SPLIT, dtype=jnp.int32))[0]
    mixed = (residual.astype(jnp.float32) + moe_out).astype(jnp.bfloat16)
    return (mixed, new_kv)
```

```python
import functools
import math

import jax
import jax.numpy as jnp
from jax import lax
from jax.experimental import pallas as pl
from jax.experimental.pallas import tpu as pltpu
from jax.sharding import PartitionSpec as P

HD = 128
SPLIT = 2
EPSILON = 1e-05
THETA = 10000.0
LOW = -1e30
ROWS = 256
KEYS = 1024
VMEM_LIMIT = 56 * 1024 * 1024


def rms_scale(inputs, gain):
    values = inputs.astype(jnp.float32)
    mean_square = jnp.mean(values * values, axis=-1, keepdims=True)
    return (values * lax.rsqrt(mean_square + EPSILON) * gain).astype(jnp.bfloat16)


def rotation_tables(positions):
    half = HD // 2
    steps = jnp.arange(half, dtype=jnp.float32)
    frequency = jnp.exp(steps * (-2.0 * math.log(THETA) / HD))
    angles = positions.astype(jnp.float32)[:, None] * frequency[None, :]
    cosine = jnp.cos(angles)
    sine = jnp.sin(angles)
    return (
        jnp.concatenate([cosine, cosine], axis=1),
        jnp.concatenate([-sine, sine], axis=1),
    )


def scores_of(query, keys):
    return lax.dot_general(
        query, keys, (((1,), (1,)), ((), ())), preferred_element_type=jnp.float32
    )


def fold(state, scores, values, factor):
    old_max, old_total, running = state
    new_max = jnp.maximum(old_max, jnp.max(scores, axis=1, keepdims=True))
    shrink = jnp.exp2((old_max - new_max) * factor)
    weights = jnp.exp2((scores - new_max) * factor)
    total = old_total * shrink + jnp.sum(weights, axis=1, keepdims=True)
    running = running * shrink + jnp.dot(
        weights.astype(jnp.bfloat16), values, preferred_element_type=jnp.float32
    )
    return new_max, total, running


def attention_kernel(
    dec_len_ref,
    pre_pos_ref,
    rows_ref,
    weight_ref,
    cos_ref,
    sin_ref,
    dec_k_ref,
    dec_v_ref,
    pre_k_ref,
    pre_v_ref,
    attended_ref,
    new_ref,
    own_k,
    own_v,
):
    dec_count = dec_k_ref.shape[0]
    block = pl.program_id(0)
    factor = math.log2(math.e) / math.sqrt(HD)
    mixed = jnp.dot(rows_ref[...], weight_ref[...], preferred_element_type=jnp.float32)
    cosine = cos_ref[...]
    sine = sin_ref[...]

    def rotated(values):
        return (values * cosine + pltpu.roll(values, HD // 2, 1) * sine).astype(jnp.bfloat16)

    query = rotated(mixed[:, :HD])
    keys = rotated(mixed[:, HD : 2 * HD])
    values = mixed[:, 2 * HD :].astype(jnp.bfloat16)
    new_ref[0] = keys
    new_ref[1] = values
    own_k[block] = keys
    own_v[block] = values

    row = lax.broadcasted_iota(jnp.int32, (ROWS, ROWS), 0)
    col = lax.broadcasted_iota(jnp.int32, (ROWS, ROWS), 1)
    first = jnp.where(block == 0, dec_count, 0)
    scores = jnp.where((col <= row) & (col >= first), scores_of(query, keys), LOW)
    state = fold(
        (
            jnp.full((ROWS, 1), LOW, jnp.float32),
            jnp.zeros((ROWS, 1), jnp.float32),
            jnp.zeros((ROWS, HD), jnp.float32),
        ),
        scores,
        values,
        factor,
    )

    def own_step(index, state):
        scores = jnp.where(
            col >= dec_count - index * ROWS, scores_of(query, own_k[index]), LOW
        )
        return fold(state, scores, own_v[index], factor)

    state = lax.fori_loop(0, block, own_step, state)
    length = pre_pos_ref[0]
    whole = length // KEYS

    def prefix_step(index, state):
        at = pl.ds(pl.multiple_of(index * KEYS, KEYS), KEYS)
        return fold(state, scores_of(query, pre_k_ref[at, :]), pre_v_ref[at, :], factor)

    def last_step(index, state):
        at = pl.ds(pl.multiple_of(index * KEYS, KEYS), KEYS)
        slot = lax.broadcasted_iota(jnp.int32, (ROWS, KEYS), 1) + index * KEYS
        scores = jnp.where(slot < length, scores_of(query, pre_k_ref[at, :]), LOW)
        return fold(state, scores, pre_v_ref[at, :], factor)

    state = lax.fori_loop(0, whole, prefix_step, state)
    state = lax.fori_loop(whole, pl.cdiv(length, KEYS), last_step, state)
    attended_ref[...] = (state[2] / state[1]).astype(jnp.bfloat16)

    @pl.when(block == 0)
    def _():
        head = 16
        few = query[:head]
        few_k = keys[:head].astype(jnp.float32)
        few_v = values[:head].astype(jnp.float32)
        own_scores = jnp.sum(few.astype(jnp.float32) * few_k, axis=1, keepdims=True)
        result = attended_ref[0:head, :].astype(jnp.float32)
        at_row = lax.broadcasted_iota(jnp.int32, (head, HD), 0)
        cache = dec_k_ref.shape[1]
        slot = lax.broadcasted_iota(jnp.int32, (head, cache), 1)
        for request in range(dec_count):
            scores = jnp.where(
                slot < dec_len_ref[request], scores_of(few, dec_k_ref[request]), LOW
            )
            highest = jnp.maximum(jnp.max(scores, axis=1, keepdims=True), own_scores)
            weights = jnp.exp2((scores - highest) * factor)
            own_weight = jnp.exp2((own_scores - highest) * factor)
            total = jnp.sum(weights, axis=1, keepdims=True) + own_weight
            summed = jnp.dot(
                weights.astype(jnp.bfloat16),
                dec_v_ref[request],
                preferred_element_type=jnp.float32,
            )
            summed = summed + own_weight.astype(jnp.bfloat16).astype(jnp.float32) * few_v
            result = jnp.where(at_row == request, summed / total, result)
        attended_ref[0:head, :] = result.astype(jnp.bfloat16)


def attention(rows, weight, cosine, sine, dec_k, dec_v, pre_k, pre_v, dec_len, pre_pos):
    count, width = rows.shape
    blocks = count // ROWS
    whole = lambda: pl.BlockSpec(memory_space=pltpu.VMEM)
    spec = pltpu.PrefetchScalarGridSpec(
        num_scalar_prefetch=2,
        grid=(blocks,),
        in_specs=[
            pl.BlockSpec((ROWS, width), lambda i, *_: (i, 0)),
            whole(),
            pl.BlockSpec((ROWS, HD), lambda i, *_: (i, 0)),
            pl.BlockSpec((ROWS, HD), lambda i, *_: (i, 0)),
            whole(),
            whole(),
            whole(),
            whole(),
        ],
        out_specs=[
            pl.BlockSpec((ROWS, HD), lambda i, *_: (i, 0)),
            pl.BlockSpec((2, ROWS, HD), lambda i, *_: (0, i, 0)),
        ],
        scratch_shapes=[
            pltpu.VMEM((blocks, ROWS, HD), jnp.bfloat16),
            pltpu.VMEM((blocks, ROWS, HD), jnp.bfloat16),
        ],
    )
    return pl.pallas_call(
        attention_kernel,
        grid_spec=spec,
        out_shape=[
            jax.ShapeDtypeStruct((count, HD), jnp.bfloat16),
            jax.ShapeDtypeStruct((2, count, HD), jnp.bfloat16),
        ],
        compiler_params=pltpu.CompilerParams(
            dimension_semantics=("arbitrary",), vmem_limit_bytes=VMEM_LIMIT
        ),
        cost_estimate=pl.CostEstimate(
            flops=2 * count * width * 3 * HD + 4 * count * 5120 * HD,
            bytes_accessed=24 * 1024 * 1024,
            transcendentals=count * 5120,
        ),
        name="attend",
    )(dec_len, pre_pos, rows, weight, cosine, sine, dec_k, dec_v, pre_k, pre_v)


def body(
    hidden,
    attn_gain,
    w_query,
    w_keyval,
    k_pool,
    v_pool,
    dec_len,
    dec_pages,
    pre_pos,
    pre_pages,
    w_out,
    moe_gain,
    expert_ids,
    router_logits,
    w_in,
    w_down,
):
    local_rows, width = hidden.shape
    req_count = lax.axis_size("req")
    exp_count = lax.axis_size("exp")
    devices = req_count * exp_count
    group_rows = local_rows * exp_count
    dec_count = dec_len.shape[0]
    page_size = k_pool.shape[1]
    normed_attn = rms_scale(hidden, attn_gain)
    joined = jnp.concatenate([w_query, w_keyval[0], w_keyval[1]], axis=1)
    row_index = jnp.arange(group_rows, dtype=jnp.int32)
    positions = pre_pos[0] + row_index - dec_count
    for request in range(dec_count):
        positions = jnp.where(row_index == request, dec_len[request], positions)
    cosine, sine = rotation_tables(positions)
    cache_len = dec_pages.shape[1] * page_size
    dec_k = k_pool[dec_pages].reshape(dec_count, cache_len, HD)
    dec_v = v_pool[dec_pages].reshape(dec_count, cache_len, HD)
    pre_k = k_pool[pre_pages[0]].reshape(-1, HD)
    pre_v = v_pool[pre_pages[0]].reshape(-1, HD)

    experts = devices // SPLIT
    top = expert_ids.shape[1]
    capacity = 2 * ((local_rows * top * 5 + 8 * experts - 1) // (8 * experts))
    gates = jax.nn.softmax(router_logits, axis=-1)
    expert_index = jnp.arange(experts, dtype=jnp.int32)
    chosen = expert_ids[:, :, None] == expert_index[None, None, :]
    named = jnp.sum(chosen.astype(jnp.float32), axis=1)
    gate_of = jnp.sum(jnp.where(chosen, gates[:, :, None], 0.0), axis=1)
    token = jnp.arange(local_rows, dtype=jnp.int32)
    earlier = (token[None, :] < token[:, None]).astype(jnp.bfloat16)
    place = jnp.dot(earlier, named.astype(jnp.bfloat16), preferred_element_type=jnp.float32)
    place = jnp.where(named > 0, place, -1.0)
    slot = jnp.arange(capacity, dtype=jnp.int32).astype(jnp.float32)
    taken = place.T[:, None, :] == slot[None, :, None]
    pick = taken.astype(jnp.bfloat16).reshape(experts * capacity, local_rows)
    merge = jnp.where(place[:, :, None] == slot[None, None, :], gate_of[:, :, None], 0.0)

    rows, cosine, sine, dec_k, dec_v, pre_k, pre_v, joined = lax.optimization_barrier(
        (
            lax.all_gather(normed_attn, "exp", axis=0, tiled=True),
            cosine,
            sine,
            dec_k,
            dec_v,
            pre_k,
            pre_v,
            joined,
        )
    )
    later_w_out, rows = lax.optimization_barrier((w_out, rows))
    full_w_out = lax.all_gather(later_w_out, "exp", axis=0, tiled=True)
    attended, new_kv = attention(
        rows, joined, cosine, sine, dec_k, dec_v, pre_k, pre_v, dec_len, pre_pos
    )
    by_head = lax.all_to_all(
        attended.reshape(exp_count, local_rows, HD), "exp", split_axis=0, concat_axis=0, tiled=True
    )
    own_heads = jnp.swapaxes(by_head, 0, 1).reshape(local_rows, exp_count * HD)
    projected = jnp.dot(own_heads, full_w_out, preferred_element_type=jnp.float32)
    residual = (hidden.astype(jnp.float32) + projected).astype(jnp.bfloat16)
    normed_moe = rms_scale(residual, moe_gain)

    outgoing = jnp.dot(pick, normed_moe, preferred_element_type=jnp.float32).astype(jnp.bfloat16)
    doubled = jnp.broadcast_to(
        outgoing.reshape(experts, 1, capacity, width), (experts, SPLIT, capacity, width)
    ).reshape(devices, capacity, width)
    arrived = lax.all_to_all(doubled, ("req", "exp"), split_axis=0, concat_axis=0, tiled=True)
    piece_units = w_down.shape[1]
    inner = jnp.dot(
        arrived.reshape(devices * capacity, width), w_in[0], preferred_element_type=jnp.float32
    )
    activated = (jax.nn.silu(inner[:, :piece_units]) * inner[:, piece_units:]).astype(jnp.bfloat16)
    partial_value = (
        jnp.dot(activated, w_down[0], preferred_element_type=jnp.float32)
        .astype(jnp.bfloat16)
        .reshape(devices, capacity, width)
    )
    returned = lax.all_to_all(
        partial_value, ("req", "exp"), split_axis=0, concat_axis=0, tiled=True
    ).reshape(devices * capacity, width)
    coarse = merge.astype(jnp.bfloat16)
    fine = (merge - coarse.astype(jnp.float32)).astype(jnp.bfloat16)
    weights = jnp.concatenate([coarse, fine], axis=0).reshape(2 * local_rows, experts, 1, capacity)
    weights = jnp.broadcast_to(
        weights, (2 * local_rows, experts, SPLIT, capacity)
    ).reshape(2 * local_rows, devices * capacity)
    summed = jnp.dot(weights, returned, preferred_element_type=jnp.float32)
    moe_out = summed[:local_rows] + summed[local_rows:]
    mixed = (residual.astype(jnp.float32) + moe_out).astype(jnp.bfloat16)
    return (mixed, new_kv)


def solution(mesh):
    placed = (
        P(("req", "exp"), None),
        P(),
        P(None, "exp"),
        P(None, None, "exp"),
        P("req", None, "exp"),
        P("req", None, "exp"),
        P("req"),
        P("req", None),
        P("req"),
        P("req", None),
        P("exp", None),
        P(),
        P(("req", "exp"), None),
        P(("req", "exp"), None),
        P(("req", "exp"), None, None),
        P(("req", "exp"), None, None),
    )
    return jax.shard_map(
        body,
        mesh=mesh,
        in_specs=placed,
        out_specs=(P(("req", "exp"), None), P(None, "req", "exp")),
        check_vma=False,
    )
```

```python
import functools
import math

import jax
import jax.numpy as jnp
from jax import lax
from jax.experimental import pallas as pl
from jax.experimental.pallas import tpu as pltpu
from jax.sharding import PartitionSpec as P

HD = 128
SPLIT = 2
EPSILON = 1e-05
THETA = 10000.0
LOW = -1e30
ROWS = 256
CHAINS = 2
STEP_ROWS = ROWS * CHAINS
KEYS = 1024
VMEM_LIMIT = 56 * 1024 * 1024


def rms_scale(inputs, gain):
    values = inputs.astype(jnp.float32)
    mean_square = jnp.mean(values * values, axis=-1, keepdims=True)
    return (values * lax.rsqrt(mean_square + EPSILON) * gain).astype(jnp.bfloat16)


def rotation_tables(positions):
    half = HD // 2
    steps = jnp.arange(half, dtype=jnp.float32)
    frequency = jnp.exp(steps * (-2.0 * math.log(THETA) / HD))
    angles = positions.astype(jnp.float32)[:, None] * frequency[None, :]
    cosine = jnp.cos(angles)
    sine = jnp.sin(angles)
    return (
        jnp.concatenate([cosine, cosine], axis=1),
        jnp.concatenate([-sine, sine], axis=1),
    )


def scores_of(query, keys):
    return lax.dot_general(
        query, keys, (((1,), (1,)), ((), ())), preferred_element_type=jnp.float32
    )


def fold(state, scores, values, factor):
    old_max, old_total, running = state
    new_max = jnp.maximum(old_max, jnp.max(scores, axis=1, keepdims=True))
    shrink = jnp.exp2((old_max - new_max) * factor)
    weights = jnp.exp2((scores - new_max) * factor)
    total = old_total * shrink + jnp.sum(weights, axis=1, keepdims=True)
    running = running * shrink + jnp.dot(
        weights.astype(jnp.bfloat16), values, preferred_element_type=jnp.float32
    )
    return new_max, total, running


def attention_kernel(
    dec_len_ref,
    pre_pos_ref,
    rows_ref,
    weight_ref,
    cos_ref,
    sin_ref,
    dec_k_ref,
    dec_v_ref,
    pre_k_ref,
    pre_v_ref,
    attended_ref,
    new_ref,
    own_k,
    own_v,
):
    dec_count = dec_k_ref.shape[0]
    block = pl.program_id(0)
    factor = math.log2(math.e) / math.sqrt(HD)
    mixed = jnp.dot(rows_ref[...], weight_ref[...], preferred_element_type=jnp.float32)
    cosine = cos_ref[...]
    sine = sin_ref[...]

    def rotated(values):
        return (values * cosine + pltpu.roll(values, HD // 2, 1) * sine).astype(jnp.bfloat16)

    query = rotated(mixed[:, :HD])
    keys = rotated(mixed[:, HD : 2 * HD])
    values = mixed[:, 2 * HD :].astype(jnp.bfloat16)
    new_ref[0] = keys
    new_ref[1] = values
    own_k[block] = keys
    own_v[block] = values
    chains = [query[i * ROWS : (i + 1) * ROWS] for i in range(CHAINS)]
    first = jnp.where(block == 0, dec_count, 0)
    states = []
    for i, part in enumerate(chains):
        span = (i + 1) * ROWS
        row = lax.broadcasted_iota(jnp.int32, (ROWS, span), 0) + i * ROWS
        col = lax.broadcasted_iota(jnp.int32, (ROWS, span), 1)
        scores = jnp.where((col <= row) & (col >= first), scores_of(part, keys[:span]), LOW)
        start = (
            jnp.full((ROWS, 1), LOW, jnp.float32),
            jnp.zeros((ROWS, 1), jnp.float32),
            jnp.zeros((ROWS, HD), jnp.float32),
        )
        states.append(fold(start, scores, values[:span], factor))

    def own_step(index, states):
        col = lax.broadcasted_iota(jnp.int32, (1, STEP_ROWS), 1)
        bias = jnp.where(col >= dec_count - index * STEP_ROWS, 0.0, LOW)
        held_k = own_k[index]
        held_v = own_v[index]
        return [
            fold(state, scores_of(part, held_k) + bias, held_v, factor)
            for part, state in zip(chains, states)
        ]

    states = lax.fori_loop(0, block, own_step, states)
    length = pre_pos_ref[0]
    whole = length // KEYS

    def prefix_step(index, states):
        at = pl.ds(pl.multiple_of(index * KEYS, KEYS), KEYS)
        held_k = pre_k_ref[at, :]
        held_v = pre_v_ref[at, :]
        return [
            fold(state, scores_of(part, held_k), held_v, factor)
            for part, state in zip(chains, states)
        ]

    def last_step(index, states):
        at = pl.ds(pl.multiple_of(index * KEYS, KEYS), KEYS)
        slot = lax.broadcasted_iota(jnp.int32, (1, KEYS), 1) + index * KEYS
        bias = jnp.where(slot < length, 0.0, LOW)
        held_k = pre_k_ref[at, :]
        held_v = pre_v_ref[at, :]
        return [
            fold(state, scores_of(part, held_k) + bias, held_v, factor)
            for part, state in zip(chains, states)
        ]

    states = lax.fori_loop(0, whole, prefix_step, states)
    states = lax.fori_loop(whole, pl.cdiv(length, KEYS), last_step, states)
    for i, state in enumerate(states):
        attended_ref[i * ROWS : (i + 1) * ROWS, :] = (state[2] / state[1]).astype(jnp.bfloat16)

    @pl.when(block == 0)
    def _():
        head = 16
        few = query[:head]
        few_k = keys[:head].astype(jnp.float32)
        few_v = values[:head].astype(jnp.float32)
        own_scores = jnp.sum(few.astype(jnp.float32) * few_k, axis=1, keepdims=True)
        result = attended_ref[0:head, :].astype(jnp.float32)
        at_row = lax.broadcasted_iota(jnp.int32, (head, HD), 0)
        cache = dec_k_ref.shape[1]
        slot = lax.broadcasted_iota(jnp.int32, (head, cache), 1)
        for request in range(dec_count):
            scores = jnp.where(
                slot < dec_len_ref[request], scores_of(few, dec_k_ref[request]), LOW
            )
            highest = jnp.maximum(jnp.max(scores, axis=1, keepdims=True), own_scores)
            weights = jnp.exp2((scores - highest) * factor)
            own_weight = jnp.exp2((own_scores - highest) * factor)
            total = jnp.sum(weights, axis=1, keepdims=True) + own_weight
            summed = jnp.dot(
                weights.astype(jnp.bfloat16),
                dec_v_ref[request],
                preferred_element_type=jnp.float32,
            )
            summed = summed + own_weight.astype(jnp.bfloat16).astype(jnp.float32) * few_v
            result = jnp.where(at_row == request, summed / total, result)
        attended_ref[0:head, :] = result.astype(jnp.bfloat16)


def attention(rows, weight, cosine, sine, dec_k, dec_v, pre_k, pre_v, dec_len, pre_pos):
    count, width = rows.shape
    blocks = count // STEP_ROWS
    whole = lambda: pl.BlockSpec(memory_space=pltpu.VMEM)
    spec = pltpu.PrefetchScalarGridSpec(
        num_scalar_prefetch=2,
        grid=(blocks,),
        in_specs=[
            pl.BlockSpec((STEP_ROWS, width), lambda i, *_: (i, 0)),
            whole(),
            pl.BlockSpec((STEP_ROWS, HD), lambda i, *_: (i, 0)),
            pl.BlockSpec((STEP_ROWS, HD), lambda i, *_: (i, 0)),
            whole(),
            whole(),
            whole(),
            whole(),
        ],
        out_specs=[
            pl.BlockSpec((STEP_ROWS, HD), lambda i, *_: (i, 0)),
            pl.BlockSpec((2, STEP_ROWS, HD), lambda i, *_: (0, i, 0)),
        ],
        scratch_shapes=[
            pltpu.VMEM((blocks, STEP_ROWS, HD), jnp.bfloat16),
            pltpu.VMEM((blocks, STEP_ROWS, HD), jnp.bfloat16),
        ],
    )
    return pl.pallas_call(
        attention_kernel,
        grid_spec=spec,
        out_shape=[
            jax.ShapeDtypeStruct((count, HD), jnp.bfloat16),
            jax.ShapeDtypeStruct((2, count, HD), jnp.bfloat16),
        ],
        compiler_params=pltpu.CompilerParams(
            dimension_semantics=("arbitrary",), vmem_limit_bytes=VMEM_LIMIT
        ),
        cost_estimate=pl.CostEstimate(
            flops=2 * count * width * 3 * HD + 4 * count * 5120 * HD,
            bytes_accessed=24 * 1024 * 1024,
            transcendentals=count * 5120,
        ),
        name="attend",
    )(dec_len, pre_pos, rows, weight, cosine, sine, dec_k, dec_v, pre_k, pre_v)


PLANE_STEPS = (
    (2, 1), (1, 2), (2, 3), (3, 2), (2, 0), (0, 2), (1, 1), (3, 3),
    (1, 3), (3, 1), (2, 2), (1, 0), (3, 0), (0, 1), (0, 3), (0, 0),
)
STEPS = [(dz, dy, (i + turn) % 2) for turn in (1, 0) for i, (dz, dy) in enumerate(PLANE_STEPS)]
STEPS.remove((0, 0, 0))
GROUP_STEPS = PLANE_STEPS[:-1]
SIDE = 4


def expert_peer(step):
    dz, dy, dx = step
    req = lax.axis_index("req")
    exp = lax.axis_index("exp")
    z, core, y, x = req // 2, req % 2, exp // SIDE, exp % SIDE
    inner = ((x + 1) // 2) % 2
    pz, py, at = (z + dz) % SIDE, (y + dy) % SIDE, (x // 2 + dx) % 2
    px = inner * (1 + at) + (1 - inner) * 3 * at
    return (pz * SIDE + py) * 2 + at, (pz * 2 + core, py * SIDE + px)


def group_peer(step):
    dy, dx = step
    exp = lax.axis_index("exp")
    place = (exp // SIDE + dy) % SIDE * SIDE + (exp % SIDE + dx) % SIDE
    return place, (lax.axis_index("req"), place)


def exchange_kernel(peer, steps, blocks_ref, out_ref, send_sem, recv_sem, local_sem):
    me, _ = peer((0,) * len(steps[0]))
    barrier = pltpu.get_barrier_semaphore()
    for step in steps:
        pl.semaphore_signal(
            barrier, inc=1, device_id=peer(step)[1], device_id_type=pl.DeviceIdType.MESH
        )
    own = pltpu.make_async_copy(blocks_ref.at[me], out_ref.at[me], local_sem)
    own.start()
    pl.semaphore_wait(barrier, len(steps))
    copies = []
    for index, step in enumerate(steps):
        place, device = peer(step)
        copy = pltpu.make_async_remote_copy(
            src_ref=blocks_ref.at[place],
            dst_ref=out_ref.at[me],
            send_sem=send_sem.at[index],
            recv_sem=recv_sem.at[index],
            device_id=device,
            device_id_type=pl.DeviceIdType.MESH,
        )
        copy.start()
        copies.append(copy)
    own.wait()
    for copy in copies:
        copy.wait()


def exchange(blocks, peer, steps, number):
    return pl.pallas_call(
        functools.partial(exchange_kernel, peer, steps),
        in_specs=[pl.BlockSpec(memory_space=pl.ANY)],
        out_specs=pl.BlockSpec(memory_space=pl.ANY),
        out_shape=jax.ShapeDtypeStruct(blocks.shape, blocks.dtype),
        scratch_shapes=[
            pltpu.SemaphoreType.DMA((len(steps),)),
            pltpu.SemaphoreType.DMA((len(steps),)),
            pltpu.SemaphoreType.DMA,
        ],
        compiler_params=pltpu.CompilerParams(collective_id=number, has_side_effects=True),
        name="exchange",
    )(blocks)


def expert_kernel(rows_ref, in_a_ref, in_b0_ref, in_b1_ref, down_a_ref, down_b_ref, out_ref):
    rows = rows_ref[...]
    depth = in_b0_ref.shape[0]
    units = down_a_ref.shape[0]

    def activate(inner):
        return (jax.nn.silu(inner[:, :units]) * inner[:, units:]).astype(jnp.bfloat16)

    inner_a = jnp.dot(rows, in_a_ref[...], preferred_element_type=jnp.float32)
    inner_b = jnp.dot(
        rows[:, :depth], in_b0_ref[...], preferred_element_type=jnp.float32
    ) + jnp.dot(rows[:, depth:], in_b1_ref[...], preferred_element_type=jnp.float32)
    total = jnp.dot(
        activate(inner_a), down_a_ref[...], preferred_element_type=jnp.float32
    ) + jnp.dot(activate(inner_b), down_b_ref[...], preferred_element_type=jnp.float32)
    out_ref[...] = total.astype(jnp.bfloat16)


def expert_rows(rows, *pieces):
    count, width = rows.shape
    whole = lambda: pl.BlockSpec(memory_space=pltpu.VMEM)
    return pl.pallas_call(
        expert_kernel,
        grid=(count // ROWS,),
        in_specs=[pl.BlockSpec((ROWS, width), lambda i: (i, 0))] + [whole() for _ in pieces],
        out_specs=pl.BlockSpec((ROWS, width), lambda i: (i, 0)),
        out_shape=jax.ShapeDtypeStruct((count, width), jnp.bfloat16),
        compiler_params=pltpu.CompilerParams(
            dimension_semantics=("arbitrary",), vmem_limit_bytes=VMEM_LIMIT
        ),
        cost_estimate=pl.CostEstimate(
            flops=2 * count * width * 3072,
            bytes_accessed=24 * 1024 * 1024,
            transcendentals=count * 1024,
        ),
        name="experts",
    )(rows, *pieces)


def body(
    hidden,
    attn_gain,
    w_query,
    w_keyval,
    k_pool,
    v_pool,
    dec_len,
    dec_pages,
    pre_pos,
    pre_pages,
    w_out,
    moe_gain,
    expert_ids,
    router_logits,
    w_in,
    w_down,
):
    local_rows, width = hidden.shape
    req_count = lax.axis_size("req")
    exp_count = lax.axis_size("exp")
    devices = req_count * exp_count
    group_rows = local_rows * exp_count
    dec_count = dec_len.shape[0]
    page_size = k_pool.shape[1]
    normed_attn = rms_scale(hidden, attn_gain)
    joined = jnp.concatenate([w_query, w_keyval[0], w_keyval[1]], axis=1)
    row_index = jnp.arange(group_rows, dtype=jnp.int32)
    positions = pre_pos[0] + row_index - dec_count
    for request in range(dec_count):
        positions = jnp.where(row_index == request, dec_len[request], positions)
    cosine, sine = rotation_tables(positions)
    cache_len = dec_pages.shape[1] * page_size
    dec_k = k_pool[dec_pages].reshape(dec_count, cache_len, HD)
    dec_v = v_pool[dec_pages].reshape(dec_count, cache_len, HD)
    pre_k = k_pool[pre_pages[0]].reshape(-1, HD)
    pre_v = v_pool[pre_pages[0]].reshape(-1, HD)

    core = lax.axis_index("req") % 2
    mates = [(i, i + 1 - 2 * (i % 2)) for i in range(req_count)]
    halves = [(i, i + 1 - 2 * (i % 2)) for i in range(exp_count)]
    experts = devices // SPLIT
    peers = experts // 2
    top = expert_ids.shape[1]
    capacity = 2 * ((local_rows * top * 5 + 8 * experts - 1) // (8 * experts))
    both_ids = jnp.concatenate([expert_ids, lax.ppermute(expert_ids, "req", mates)], axis=0)
    both_logits = jnp.concatenate(
        [router_logits, lax.ppermute(router_logits, "req", mates)], axis=0
    )
    gates = jax.nn.softmax(both_logits, axis=-1)
    plane = exp_count // SPLIT
    peer_index = jnp.arange(peers, dtype=jnp.int32)
    expert_index = (peer_index // plane * 2 + core) * plane + peer_index % plane
    chosen = both_ids[:, :, None] == expert_index[None, None, :]
    named = jnp.sum(chosen.astype(jnp.float32), axis=1)
    gate_of = jnp.sum(jnp.where(chosen, gates[:, :, None], 0.0), axis=1)
    token = jnp.arange(2 * local_rows, dtype=jnp.int32)
    same = token[None, :] // local_rows == token[:, None] // local_rows
    earlier = ((token[None, :] < token[:, None]) & same).astype(jnp.bfloat16)
    place = jnp.dot(earlier, named.astype(jnp.bfloat16), preferred_element_type=jnp.float32)
    place = place + jnp.where(token >= local_rows, float(capacity), 0.0)[:, None]
    place = jnp.where(named > 0, place, -1.0)
    block = 2 * capacity
    slot = jnp.arange(block, dtype=jnp.int32).astype(jnp.float32)
    taken = place.T[:, None, :] == slot[None, :, None]
    pick = taken.astype(jnp.bfloat16).reshape(peers * block, 2 * local_rows)
    merge = jnp.where(place[:, :, None] == slot[None, None, :], gate_of[:, :, None], 0.0)
    merge = merge.reshape(2 * local_rows, peers * block)
    coarse = merge.astype(jnp.bfloat16)
    fine = (merge - coarse.astype(jnp.float32)).astype(jnp.bfloat16)
    weights = jnp.concatenate([coarse, fine], axis=0)

    depth = width // 4
    rows, cosine, sine, dec_k, dec_v, pre_k, pre_v, joined, pick, weights = lax.optimization_barrier(
        (
            lax.all_gather(normed_attn, "exp", axis=0, tiled=True),
            cosine,
            sine,
            dec_k,
            dec_v,
            pre_k,
            pre_v,
            joined,
            pick,
            weights,
        )
    )
    half = HD // 2
    own_half = lax.dynamic_slice_in_dim(w_out, core * half, half, 0)
    later_w_out, later_in, rows = lax.optimization_barrier((own_half, w_in[0, :depth], rows))
    near_w_out = lax.all_gather(later_w_out, "exp", axis=0, tiled=True)
    other_in_0 = lax.ppermute(later_in, "exp", halves)
    attended, new_kv = attention(
        rows, joined, cosine, sine, dec_k, dec_v, pre_k, pre_v, dec_len, pre_pos
    )
    attended, near_w_out, other_in_0 = lax.optimization_barrier(
        (attended, near_w_out, other_in_0)
    )
    far_w_out = lax.ppermute(near_w_out, "req", mates)
    by_head = exchange(
        attended.reshape(exp_count, local_rows, HD), group_peer, GROUP_STEPS, 2
    )
    later_in, later_down, by_head = lax.optimization_barrier(
        (w_in[0, depth:], w_down[0], by_head)
    )
    other_in_1 = lax.ppermute(later_in, "exp", halves)
    other_down = lax.ppermute(later_down, "exp", halves)
    first_half = jnp.swapaxes(by_head[:, :, :half], 0, 1).reshape(local_rows, -1)
    second_half = jnp.swapaxes(by_head[:, :, half:], 0, 1).reshape(local_rows, -1)
    near = jnp.where(core == 0, first_half, second_half)
    far = jnp.where(core == 0, second_half, first_half)
    projected = jnp.dot(near, near_w_out, preferred_element_type=jnp.float32) + jnp.dot(
        far, far_w_out, preferred_element_type=jnp.float32
    )
    residual = (hidden.astype(jnp.float32) + projected).astype(jnp.bfloat16)
    normed_moe = rms_scale(residual, moe_gain)

    both_rows = jnp.concatenate([normed_moe, lax.ppermute(normed_moe, "req", mates)], axis=0)
    outgoing = jnp.dot(pick, both_rows, preferred_element_type=jnp.float32).astype(jnp.bfloat16)
    arrived = exchange(outgoing.reshape(peers, block, width), expert_peer, STEPS, 0)
    partial_value = expert_rows(
        arrived.reshape(peers * block, width), w_in[0], other_in_0, other_in_1, w_down[0], other_down
    )
    returned = exchange(partial_value.reshape(peers, block, width), expert_peer, STEPS, 1)
    summed = jnp.dot(
        weights, returned.reshape(peers * block, width), preferred_element_type=jnp.float32
    )
    summed = summed[: 2 * local_rows] + summed[2 * local_rows :]
    theirs = lax.ppermute(summed[local_rows:].astype(jnp.bfloat16), "req", mates)
    moe_out = summed[:local_rows] + theirs.astype(jnp.float32)
    mixed = (residual.astype(jnp.float32) + moe_out).astype(jnp.bfloat16)
    return (mixed, new_kv)


def solution(mesh):
    placed = (
        P(("req", "exp"), None),
        P(),
        P(None, "exp"),
        P(None, None, "exp"),
        P("req", None, "exp"),
        P("req", None, "exp"),
        P("req"),
        P("req", None),
        P("req"),
        P("req", None),
        P("exp", None),
        P(),
        P(("req", "exp"), None),
        P(("req", "exp"), None),
        P(("req", "exp"), None, None),
        P(("req", "exp"), None, None),
    )
    return jax.shard_map(
        body,
        mesh=mesh,
        in_specs=placed,
        out_specs=(P(("req", "exp"), None), P(None, "req", "exp")),
        check_vma=False,
    )
```
